32 devices in a mesh: rep: 2 (over y), tp: 4 (over z), fs: 4 (over x, core).
Axes of the slice: x: 2, y: 2, z: 4, core: 2. Of those that a mesh axis runs over, the one named last changes fastest.
Arguments:
- hidden: bfloat16 [16, 8192], P(('rep', 'fs'), 'tp'), may hold values from -6 to 6
- cache_key: bfloat16 [16, 2048, 1024], P(('rep', 'fs'), None, 'tp'), may hold values from -1300 to 1300
- cache_value: bfloat16 [16, 2048, 1024], P(('rep', 'fs'), None, 'tp'), may hold values from -6 to 6
- lengths: int32 [16], P(('rep', 'fs')), may hold values from 8 to 2047
- owner: int32 [1], replicated, may hold values from 0 to 8191
- query_weight: bfloat16 [2, 8192, 4096], P('rep', 'fs', 'tp'), may hold values from -0.0625 to 0.0625
- key_weight: bfloat16 [2, 8192, 1024], P('rep', 'fs', 'tp'), may hold values from -0.0625 to 0.0625
- value_weight: bfloat16 [2, 8192, 1024], P('rep', 'fs', 'tp'), may hold values from -0.0625 to 0.0625
- out_weight: bfloat16 [2, 4096, 8192], P('rep', 'tp', 'fs'), may hold values from -0.09375 to 0.09375
Outputs:
- mixed: bfloat16 [16, 8192], P(('rep', 'fs'), 'tp')
- new_key: bfloat16 [16, 1024], P(('rep', 'fs'), 'tp')
- new_value: bfloat16 [16, 1024], P(('rep', 'fs'), 'tp')
- fresh_query: bfloat16 [2, 8192, 4096], P('rep', 'fs', 'tp')
- fresh_key: bfloat16 [2, 8192, 1024], P('rep', 'fs', 'tp')
- fresh_value: bfloat16 [2, 8192, 1024], P('rep', 'fs', 'tp')
- fresh_out: bfloat16 [2, 4096, 8192], P('rep', 'tp', 'fs')
The draws below stay inside these ranges and needn't reach their ends.
Inputs may be any that keep to these rules, and one draw needn't show every extreme that they name: `lengths`: the number of positions already in each sequence's cache; the new token stands at that position.
All inputs are finite; a program needn't handle non-finite values.
Results may differ from the reference program's by a relative error of at most 0.0065.
Values may be sent and summed in bfloat16 or wider, within the bound.
A program may use at most 64 MiB of HBM per device.

```python
import jax
import jax.numpy as jnp
from jax import lax

D = 8192
HQ = 32
KVH = 8
DH = 128
CACHE = 2048
BATCH = 16
N_REP = 2


def draw_cache_key(key, part):
    full_shape = (BATCH, CACHE, KVH * DH)
    noise_field = jnp.clip(jax.random.normal(key, full_shape, jnp.float32), -6.0, 6.0)
    return noise_field.astype(jnp.bfloat16)


def place_ends(array, stream_key, least, largest):
    longest = array.shape.index(max(array.shape))
    spots = []
    for shift in (0, 1):
        where = [jax.random.randint(jax.random.fold_in(stream_key, axis), (), 0, length) for axis, length in enumerate(array.shape)]
        where[longest] = (where[longest] + shift) % array.shape[longest]
        spots.append(tuple(where))
    return array.at[spots[0]].set(least).at[spots[1]].set(largest)


def levels(key, dims, cuts, least, largest):
    level = 1.0
    for dim, blocks in cuts:
        steps = jax.random.uniform(jax.random.fold_in(jax.random.fold_in(key, 6), dim), (blocks,), jnp.float32, least / len(cuts), largest / len(cuts))
        level = level * jnp.repeat(jnp.exp(steps), dims[dim] // blocks).reshape((-1,) + (1,) * (len(dims) - 1 - dim))
    return level


def noise(stream_key, extent, scale, limit, cuts=(), held_as=jnp.bfloat16):
    result = scale * jax.random.normal(stream_key, extent, jnp.float32)
    if cuts:
        result = result * levels(stream_key, extent, cuts, -0.22, 0.18)
    return jnp.clip(result, -limit, limit).astype(held_as)


def setup_inputs(seed: int = 0) -> dict:
    keys = jax.random.split(jax.random.key(seed), 10)
    hidden = noise(keys[0], (BATCH, D), 1.0, 6.0, ((0, 8), (1, 4)))
    cache_key = draw_cache_key(jax.random.fold_in(keys[9], 71), 0)
    cache_value = noise(keys[2], (BATCH, CACHE, KVH * DH), 1.0, 6.0, ((0, 8), (2, 4)))
    lengths = place_ends(jax.random.randint(keys[3], (BATCH,), 8, CACHE), jax.random.fold_in(keys[3], 1), 8, CACHE - 1).astype(jnp.int32)
    owner = jax.random.randint(keys[4], (1,), 0, N_REP * 4096).astype(jnp.int32)
    query_weight = noise(keys[5], (N_REP, D, HQ * DH), D ** -0.5, 0.0625, ((0, 2), (1, 4), (2, 4)))
    key_weight = noise(keys[6], (N_REP, D, KVH * DH), D ** -0.5, 0.0625, ((0, 2), (1, 4), (2, 4)))
    value_weight = noise(keys[7], (N_REP, D, KVH * DH), D ** -0.5, 0.0625, ((0, 2), (1, 4), (2, 4)))
    out_weight = noise(keys[8], (N_REP, HQ * DH, D), (HQ * DH) ** -0.5, 0.09375, ((0, 2), (1, 4), (2, 4)))
    return dict(hidden=hidden, cache_key=cache_key, cache_value=cache_value, lengths=lengths, owner=owner, query_weight=query_weight, key_weight=key_weight, value_weight=value_weight, out_weight=out_weight)


rope_base = 500000.0
epsilon = 1e-05

def rotate(heads, positions):
    half_dim = heads.shape[-1] // 2
    frequency = rope_base ** (-(jnp.arange(half_dim, dtype=jnp.float32) * 2.0 / heads.shape[-1]))
    angles = positions.astype(jnp.float32)[:, None] * frequency[None, :]
    cosine = jnp.cos(angles)[:, None, :]
    sine_part = jnp.sin(angles)[:, None, :]
    first_half = heads[..., :half_dim]
    second_half = heads[..., half_dim:]
    return jnp.concatenate([first_half * cosine - second_half * sine_part, second_half * cosine + first_half * sine_part], axis=-1)

def attend_one(items):
    query, own_key, own_value, keys_seq, values_seq, length = items
    scale = DH ** (-0.5)
    keys_wide = keys_seq.astype(jnp.float32).reshape(CACHE, KVH, DH)
    values_wide = values_seq.astype(jnp.float32).reshape(CACHE, KVH, DH)
    scores = jnp.einsum('hgd,thd->hgt', query, keys_wide) * scale
    own_score = jnp.einsum('hgd,hd->hg', query, own_key) * scale
    live = jnp.arange(CACHE, dtype=jnp.int32) < length
    masked = jnp.where(live, scores, -jnp.inf)
    row_max = jnp.maximum(lax.optimization_barrier(jnp.max(masked, axis=-1)), own_score)
    weights = jnp.where(live, jnp.exp(scores - row_max[..., None]), 0.0)
    own_weight = jnp.exp(own_score - row_max)
    denominator = lax.optimization_barrier(jnp.sum(weights, axis=-1)) + own_weight
    probs = lax.optimization_barrier((weights / denominator[..., None]).astype(jnp.bfloat16)).astype(jnp.float32)
    own_prob = lax.optimization_barrier((own_weight / denominator).astype(jnp.bfloat16)).astype(jnp.float32)
    context = jnp.einsum('hgt,thd->hgd', probs, values_wide)
    return context + own_prob[..., None] * own_value[:, None, :]

def reference(hidden, cache_key, cache_value, lengths, owner, query_weight, key_weight, value_weight, out_weight):
    owner_rank = (owner[0] % N_REP).astype(jnp.int32)
    query_block = lax.dynamic_index_in_dim(query_weight, owner_rank, 0, keepdims=False)
    key_block = lax.dynamic_index_in_dim(key_weight, owner_rank, 0, keepdims=False)
    value_block = lax.dynamic_index_in_dim(value_weight, owner_rank, 0, keepdims=False)
    out_block = lax.dynamic_index_in_dim(out_weight, owner_rank, 0, keepdims=False)
    hidden_wide = hidden.astype(jnp.float32)
    normed = (hidden_wide * lax.rsqrt(lax.optimization_barrier(jnp.mean(hidden_wide * hidden_wide, axis=-1, keepdims=True)) + epsilon)).astype(jnp.bfloat16)
    query_proj = jnp.dot(normed, query_block, preferred_element_type=jnp.float32)
    key_proj = jnp.dot(normed, key_block, preferred_element_type=jnp.float32)
    value_proj = jnp.dot(normed, value_block, preferred_element_type=jnp.float32)
    query_rot = rotate(query_proj.reshape(BATCH, HQ, DH), lengths).astype(jnp.bfloat16)
    key_new = rotate(key_proj.reshape(BATCH, KVH, DH), lengths).astype(jnp.bfloat16)
    value_new = value_proj.astype(jnp.bfloat16).reshape(BATCH, KVH, DH)
    group_size = HQ // KVH
    query_wide = lax.optimization_barrier(query_rot).astype(jnp.float32).reshape(BATCH, KVH, group_size, DH)
    key_wide = lax.optimization_barrier(key_new).astype(jnp.float32)
    value_wide = lax.optimization_barrier(value_new).astype(jnp.float32)
    context = lax.map(attend_one, (query_wide, key_wide, value_wide, cache_key, cache_value, lengths))
    context = context.astype(jnp.bfloat16).reshape(BATCH, HQ * DH)
    summed = jnp.dot(context, out_block, preferred_element_type=jnp.float32)
    mixed = (summed + hidden_wide).astype(jnp.bfloat16)
    fresh_query = jnp.broadcast_to(query_block[None], query_weight.shape)
    fresh_key = jnp.broadcast_to(key_block[None], key_weight.shape)
    fresh_value = jnp.broadcast_to(value_block[None], value_weight.shape)
    fresh_out = jnp.broadcast_to(out_block[None], out_weight.shape)
    return (mixed, key_new.reshape(BATCH, KVH * DH), value_new.reshape(BATCH, KVH * DH), fresh_query, fresh_key, fresh_value, fresh_out)
```

```python
import jax
import jax.numpy as jnp
from jax import lax
from jax.sharding import PartitionSpec as P

DH = 128


rope_base = 500000.0
epsilon = 1e-05


def exchange(shard, axis, root):
    size = lax.axis_size(axis)
    rank = lax.axis_index(axis)
    if size & (size - 1):
        return lax.psum(jnp.where(rank == root, shard, jnp.zeros_like(shard)), axis)
    away = jnp.bitwise_xor(rank, root)
    step = 1
    while step < size:
        pairs = [(i, i ^ step) for i in range(size)]
        received = lax.ppermute(shard, axis, pairs)
        takes = (away >= step) & (away < 2 * step)
        shard = jnp.where(takes, received, shard)
        step *= 2
    return shard


def gather(shard, axis, dim):
    size = lax.axis_size(axis)
    copies = jnp.broadcast_to(shard[None], (size,) + shard.shape)
    pieces = lax.all_to_all(copies, axis, split_axis=0, concat_axis=0, tiled=True)
    return jnp.concatenate([pieces[i] for i in range(size)], axis=dim)


def scatter_sum(terms, axis):
    return jnp.sum(lax.all_to_all(terms, axis, split_axis=0, concat_axis=0, tiled=True), axis=0)


def rotate(heads, positions):
    half_dim = heads.shape[-1] // 2
    frequency = rope_base ** (-(jnp.arange(half_dim, dtype=jnp.float32) * 2.0 / heads.shape[-1]))
    angles = positions.astype(jnp.float32)[:, None] * frequency[None, :]
    cosine = jnp.cos(angles)[:, None, :]
    sine_part = jnp.sin(angles)[:, None, :]
    first_half = heads[..., :half_dim]
    second_half = heads[..., half_dim:]
    return jnp.concatenate(
        [
            first_half * cosine - second_half * sine_part,
            second_half * cosine + first_half * sine_part,
        ],
        axis=-1,
    )


def attend(query, own_key, own_value, cache_key, cache_value, lengths):
    seqs, span, width = cache_key.shape
    kv_local = query.shape[1]
    head_size = query.shape[3]
    keys_view = cache_key.reshape(seqs, span, kv_local, head_size)
    values_view = cache_value.reshape(seqs, span, kv_local, head_size)
    scale = head_size ** (-0.5)
    scores = (
        jnp.einsum("shgd,sthd->shgt", query, keys_view, preferred_element_type=jnp.float32) * scale
    )
    own_score = (
        jnp.einsum("shgd,shd->shg", query, own_key, preferred_element_type=jnp.float32) * scale
    )
    live = (jnp.arange(span, dtype=jnp.int32)[None, :] < lengths[:, None])[:, None, None, :]
    masked = jnp.where(live, scores, -jnp.inf)
    row_max = jnp.maximum(jnp.max(masked, axis=-1), own_score)
    weights = jnp.where(live, jnp.exp(scores - row_max[..., None]), 0.0)
    own_weight = jnp.exp(own_score - row_max)
    denominator = jnp.sum(weights, axis=-1) + own_weight
    probs = (weights / denominator[..., None]).astype(jnp.bfloat16)
    own_prob = (own_weight / denominator).astype(jnp.bfloat16)
    context = jnp.einsum("shgt,sthd->shgd", probs, values_view, preferred_element_type=jnp.float32)
    return (
        context
        + own_prob.astype(jnp.float32)[..., None] * own_value.astype(jnp.float32)[:, :, None, :]
    )


def local(
    hidden,
    cache_key,
    cache_value,
    lengths,
    owner,
    query_weight,
    key_weight,
    value_weight,
    out_weight,
):
    owner_rank = owner[0] % lax.axis_size("rep")
    features = gather(hidden, "tp", 1)
    hidden_wide = features.astype(jnp.float32)
    normed = (
        hidden_wide
        * lax.rsqrt(jnp.mean(hidden_wide * hidden_wide, axis=-1, keepdims=True) + epsilon)
    ).astype(jnp.bfloat16)
    fresh_query = exchange(query_weight, "rep", owner_rank)
    fresh_key = exchange(key_weight, "rep", owner_rank)
    fresh_value = exchange(value_weight, "rep", owner_rank)
    chunks = 4
    depth = out_weight.shape[1] // chunks
    out_pieces = [
        exchange(out_weight[:, i * depth : (i + 1) * depth], "rep", owner_rank)
        for i in range(chunks)
    ]
    fresh_out = out_weight
    for i in range(chunks):
        fresh_out = lax.dynamic_update_slice(fresh_out, out_pieces[i], (0, i * depth, 0))
    query_rows = fresh_query[0]
    key_rows = fresh_key[0]
    value_rows = fresh_value[0]
    seqs = normed.shape[0]
    query_width = query_rows.shape[1]
    key_width = key_rows.shape[1]
    token_block = lax.all_to_all(normed, "fs", split_axis=1, concat_axis=0, tiled=True)
    groups = lax.axis_size("fs")
    joined = scatter_sum(
        jnp.concatenate(
            [
                jnp.dot(token_block, query_rows, preferred_element_type=jnp.float32),
                jnp.dot(token_block, key_rows, preferred_element_type=jnp.float32),
                jnp.dot(token_block, value_rows, preferred_element_type=jnp.float32),
            ],
            axis=1,
        ).reshape(groups, seqs, query_width + 2 * key_width),
        "fs",
    )
    query_proj = joined[:, :query_width]
    key_proj = joined[:, query_width : query_width + key_width]
    value_proj = joined[:, query_width + key_width :]
    q_heads = query_proj.shape[1] // DH
    kv_heads = key_proj.shape[1] // DH
    query_rot = rotate(query_proj.reshape(seqs, q_heads, DH), lengths).astype(jnp.bfloat16)
    query_rot = query_rot.reshape(seqs, kv_heads, q_heads // kv_heads, DH)
    key_new = rotate(key_proj.reshape(seqs, kv_heads, DH), lengths).astype(jnp.bfloat16)
    value_new = value_proj.astype(jnp.bfloat16).reshape(seqs, kv_heads, DH)
    context = attend(query_rot, key_new, value_new, cache_key, cache_value, lengths)
    context = context.astype(jnp.bfloat16).reshape(seqs, q_heads * DH)
    group_context = gather(context, "fs", 0)
    partial_out = 0.0
    for i in range(chunks):
        partial_out = partial_out + jnp.dot(
            group_context[:, i * depth : (i + 1) * depth],
            out_pieces[i][0],
            preferred_element_type=jnp.float32,
        )
    terms = lax.all_to_all(partial_out, "fs", split_axis=0, concat_axis=1, tiled=True)
    model_groups = lax.axis_size("tp")
    terms = terms.reshape(seqs, model_groups, -1).transpose(1, 0, 2)
    summed = scatter_sum(terms, "tp")
    mixed = (summed + hidden.astype(jnp.float32)).astype(jnp.bfloat16)
    return (
        mixed,
        key_new.reshape(seqs, kv_heads * DH),
        value_new.reshape(seqs, kv_heads * DH),
        fresh_query,
        fresh_key,
        fresh_value,
        fresh_out,
    )


def solution(mesh):
    return jax.shard_map(
        local,
        mesh=mesh,
        in_specs=(
            P(("rep", "fs"), "tp"),
            P(("rep", "fs"), None, "tp"),
            P(("rep", "fs"), None, "tp"),
            P(("rep", "fs")),
            P(),
            P("rep", "fs", "tp"),
            P("rep", "fs", "tp"),
            P("rep", "fs", "tp"),
            P("rep", "tp", "fs"),
        ),
        out_specs=(
            P(("rep", "fs"), "tp"),
            P(("rep", "fs"), "tp"),
            P(("rep", "fs"), "tp"),
            P("rep", "fs", "tp"),
            P("rep", "fs", "tp"),
            P("rep", "fs", "tp"),
            P("rep", "tp", "fs"),
        ),
        check_vma=False,
    )
```

```python
import jax
import jax.numpy as jnp
from jax import lax
from jax.sharding import PartitionSpec as P

DH = 128


rope_base = 500000.0
epsilon = 1e-05


def gather(shard, axis, dim):
    pieces = spread(shard, axis)
    return jnp.concatenate([pieces[i] for i in range(pieces.shape[0])], axis=dim)


def spread(shard, axis):
    size = lax.axis_size(axis)
    copies = jnp.broadcast_to(shard[None], (size,) + shard.shape)
    return lax.all_to_all(copies, axis, split_axis=0, concat_axis=0, tiled=True)


def swap(terms, axis):
    return lax.all_to_all(terms, axis, split_axis=0, concat_axis=0, tiled=True)


FLIGHT = 3
EIGHTHS = ((3, 2, 1, 2), (8,), (8,), (2, 2, 2, 1, 1))
ORDER = (1, 2, 0, 3)


def synchronize(weights, axis, root):
    size = lax.axis_size(axis)
    rank = lax.axis_index(axis)
    if size & (size - 1):
        mine = rank == root
        return [lax.psum(jnp.where(mine, w, jnp.zeros_like(w)), axis) for w in weights]
    away = jnp.bitwise_xor(rank, root)
    fresh = list(weights)
    flying = []

    def land():
        which, start, received, takes, own = flying.pop(0)
        piece = jnp.where(takes, received, own)
        fresh[which] = lax.dynamic_update_slice(fresh[which], piece, (0, start, 0))

    step = 1
    while step < size:
        pairs = [(i, i ^ step) for i in range(size)]
        takes = (away >= step) & (away < 2 * step)
        held = list(fresh)
        for which in ORDER:
            whole = held[which]
            start = 0
            for part in EIGHTHS[which]:
                rows = whole.shape[1] * part // 8
                own = whole[:, start : start + rows]
                sent = own
                if len(flying) == FLIGHT:
                    first = flying[0]
                    sent, landed = lax.optimization_barrier((own, first[2]))
                    flying[0] = (first[0], first[1], landed) + first[3:]
                    land()
                flying.append((which, start, lax.ppermute(sent, axis, pairs), takes, own))
                start += rows
        while flying:
            land()
        step *= 2
    return fresh


def rotate(heads, positions):
    half_dim = heads.shape[-1] // 2
    frequency = rope_base ** (-(jnp.arange(half_dim, dtype=jnp.float32) * 2.0 / heads.shape[-1]))
    angles = positions.astype(jnp.float32)[:, None] * frequency[None, :]
    cosine = jnp.cos(angles)[:, None, :]
    sine_part = jnp.sin(angles)[:, None, :]
    first_half = heads[..., :half_dim]
    second_half = heads[..., half_dim:]
    return jnp.concatenate(
        [
            first_half * cosine - second_half * sine_part,
            second_half * cosine + first_half * sine_part,
        ],
        axis=-1,
    )


def attend(query, own_key, own_value, cache_key, cache_value, lengths):
    seqs, span, width = cache_key.shape
    kv_local = query.shape[1]
    head_size = query.shape[3]
    keys_view = cache_key.reshape(seqs, span, kv_local, head_size)
    values_view = cache_value.reshape(seqs, span, kv_local, head_size)
    scale = head_size ** (-0.5)
    scores = (
        jnp.einsum("shgd,sthd->shgt", query, keys_view, preferred_element_type=jnp.float32) * scale
    )
    own_score = (
        jnp.einsum("shgd,shd->shg", query, own_key, preferred_element_type=jnp.float32) * scale
    )
    live = (jnp.arange(span, dtype=jnp.int32)[None, :] < lengths[:, None])[:, None, None, :]
    masked = jnp.where(live, scores, -jnp.inf)
    row_max = jnp.maximum(jnp.max(masked, axis=-1), own_score)
    weights = jnp.where(live, jnp.exp(scores - row_max[..., None]), 0.0)
    own_weight = jnp.exp(own_score - row_max)
    denominator = jnp.sum(weights, axis=-1) + own_weight
    probs = (weights / denominator[..., None]).astype(jnp.bfloat16)
    own_prob = (own_weight / denominator).astype(jnp.bfloat16)
    context = jnp.einsum("shgt,sthd->shgd", probs, values_view, preferred_element_type=jnp.float32)
    return (
        context
        + own_prob.astype(jnp.float32)[..., None] * own_value.astype(jnp.float32)[:, :, None, :]
    )


def local(
    hidden,
    cache_key,
    cache_value,
    lengths,
    owner,
    query_weight,
    key_weight,
    value_weight,
    out_weight,
):
    groups = lax.axis_size("rep")
    members = lax.axis_size("fs")
    owner_rank = owner[0] % groups
    fresh_query, fresh_key, fresh_value, fresh_out = synchronize(
        (query_weight, key_weight, value_weight, out_weight), "rep", owner_rank
    )
    features = gather(hidden, "tp", 1)
    hidden_wide = features.astype(jnp.float32)
    normed = (
        hidden_wide
        * lax.rsqrt(jnp.mean(hidden_wide * hidden_wide, axis=-1, keepdims=True) + epsilon)
    ).astype(jnp.bfloat16)
    seqs = normed.shape[0]
    query_width = query_weight.shape[2]
    key_width = key_weight.shape[2]
    block = normed.shape[1] // members
    blocks = normed.reshape(seqs, members, block).transpose(1, 0, 2)
    blocks = jnp.broadcast_to(blocks[None], (groups,) + blocks.shape)
    tokens = swap(blocks.reshape(groups * members, seqs, block), ("rep", "fs"))
    tokens = tokens.reshape(groups * members * seqs, block)
    shares = jnp.concatenate(
        [
            jnp.dot(tokens, query_weight[0], preferred_element_type=jnp.float32),
            jnp.dot(tokens, key_weight[0], preferred_element_type=jnp.float32),
            jnp.dot(tokens, value_weight[0], preferred_element_type=jnp.float32),
        ],
        axis=1,
    ).reshape(groups * members, seqs, query_width + 2 * key_width)
    shares = swap(shares, ("rep", "fs")).reshape(groups, members, seqs, -1)
    joined = jnp.sum(lax.dynamic_index_in_dim(shares, owner_rank, 0, keepdims=False), axis=0)
    query_proj = joined[:, :query_width]
    key_proj = joined[:, query_width : query_width + key_width]
    value_proj = joined[:, query_width + key_width :]
    q_heads = query_proj.shape[1] // DH
    kv_heads = key_proj.shape[1] // DH
    query_rot = rotate(query_proj.reshape(seqs, q_heads, DH), lengths).astype(jnp.bfloat16)
    query_rot = query_rot.reshape(seqs, kv_heads, q_heads // kv_heads, DH)
    key_new = rotate(key_proj.reshape(seqs, kv_heads, DH), lengths).astype(jnp.bfloat16)
    value_new = value_proj.astype(jnp.bfloat16).reshape(seqs, kv_heads, DH)
    context = attend(query_rot, key_new, value_new, cache_key, cache_value, lengths)
    context = context.astype(jnp.bfloat16).reshape(seqs, q_heads * DH)
    all_context = spread(context, ("rep", "fs")).reshape(groups * members * seqs, q_heads * DH)
    partial_out = jnp.dot(all_context, out_weight[0], preferred_element_type=jnp.float32)
    terms = swap(partial_out.reshape(groups * members, seqs, -1), ("rep", "fs"))
    terms = terms.reshape(groups, members, seqs, -1)
    terms = lax.dynamic_index_in_dim(terms, owner_rank, 0, keepdims=False)
    terms = terms.transpose(1, 0, 2).reshape(seqs, lax.axis_size("tp"), -1).transpose(1, 0, 2)
    summed = jnp.sum(swap(terms, "tp"), axis=0)
    mixed = (summed + hidden.astype(jnp.float32)).astype(jnp.bfloat16)
    return (
        mixed,
        key_new.reshape(seqs, kv_heads * DH),
        value_new.reshape(seqs, kv_heads * DH),
        fresh_query,
        fresh_key,
        fresh_value,
        fresh_out,
    )


def solution(mesh):
    return jax.shard_map(
        local,
        mesh=mesh,
        in_specs=(
            P(("rep", "fs"), "tp"),
            P(("rep", "fs"), None, "tp"),
            P(("rep", "fs"), None, "tp"),
            P(("rep", "fs")),
            P(),
            P("rep", "fs", "tp"),
            P("rep", "fs", "tp"),
            P("rep", "fs", "tp"),
            P("rep", "tp", "fs"),
        ),
        out_specs=(
            P(("rep", "fs"), "tp"),
            P(("rep", "fs"), "tp"),
            P(("rep", "fs"), "tp"),
            P("rep", "fs", "tp"),
            P("rep", "fs", "tp"),
            P("rep", "fs", "tp"),
            P("rep", "tp", "fs"),
        ),
        check_vma=False,
    )
```

```python
import jax
import jax.numpy as jnp
from jax import lax
from jax.sharding import PartitionSpec as P

DH = 128


rope_base = 500000.0
epsilon = 1e-05


def exchange(shard, axis, root):
    size = lax.axis_size(axis)
    rank = lax.axis_index(axis)
    if size & (size - 1):
        return lax.psum(jnp.where(rank == root, shard, jnp.zeros_like(shard)), axis)
    away = jnp.bitwise_xor(rank, root)
    step = 1
    while step < size:
        pairs = [(i, i ^ step) for i in range(size)]
        received = lax.ppermute(shard, axis, pairs)
        takes = (away >= step) & (away < 2 * step)
        shard = jnp.where(takes, received, shard)
        step *= 2
    return shard


OUT_CUTS = (0, 3, 6, 8)


def gather(shard, axis, dim):
    size = lax.axis_size(axis)
    copies = jnp.broadcast_to(shard[None], (size,) + shard.shape)
    pieces = lax.all_to_all(copies, axis, split_axis=0, concat_axis=0, tiled=True)
    return jnp.concatenate([pieces[i] for i in range(size)], axis=dim)


def scatter_sum(terms, axis):
    return jnp.sum(lax.all_to_all(terms, axis, split_axis=0, concat_axis=0, tiled=True), axis=0)


def rotate(heads, positions):
    half_dim = heads.shape[-1] // 2
    frequency = rope_base ** (-(jnp.arange(half_dim, dtype=jnp.float32) * 2.0 / heads.shape[-1]))
    angles = positions.astype(jnp.float32)[:, None] * frequency[None, :]
    cosine = jnp.cos(angles)[:, None, :]
    sine_part = jnp.sin(angles)[:, None, :]
    first_half = heads[..., :half_dim]
    second_half = heads[..., half_dim:]
    return jnp.concatenate(
        [
            first_half * cosine - second_half * sine_part,
            second_half * cosine + first_half * sine_part,
        ],
        axis=-1,
    )


def attend(query, own_key, own_value, cache_key, cache_value, lengths):
    seqs, span, _ = cache_key.shape
    kv_local = query.shape[1]
    head_size = query.shape[3]
    keys_view = cache_key.reshape(seqs, span, kv_local, head_size)
    values_view = cache_value.reshape(seqs, span, kv_local, head_size)
    scale = head_size ** (-0.5)
    scores = (
        jnp.einsum("shgd,sthd->shgt", query, keys_view, preferred_element_type=jnp.float32) * scale
    )
    own_score = (
        jnp.einsum("shgd,shd->shg", query, own_key, preferred_element_type=jnp.float32) * scale
    )
    live = (jnp.arange(span, dtype=jnp.int32)[None, :] < lengths[:, None])[:, None, None, :]
    masked = jnp.where(live, scores, -jnp.inf)
    row_max = jnp.maximum(jnp.max(masked, axis=-1), own_score)
    weights = jnp.where(live, jnp.exp(scores - row_max[..., None]), 0.0)
    own_weight = jnp.exp(own_score - row_max)
    denominator = jnp.sum(weights, axis=-1) + own_weight
    probs = (weights / denominator[..., None]).astype(jnp.bfloat16)
    own_prob = (own_weight / denominator).astype(jnp.bfloat16)
    context = jnp.einsum("shgt,sthd->shgd", probs, values_view, preferred_element_type=jnp.float32)
    return (
        context
        + own_prob.astype(jnp.float32)[..., None] * own_value.astype(jnp.float32)[:, :, None, :]
    )


def local(
    hidden,
    cache_key,
    cache_value,
    lengths,
    owner,
    query_weight,
    key_weight,
    value_weight,
    out_weight,
):
    owner_rank = owner[0] % lax.axis_size("rep")
    features = gather(hidden, "tp", 1)
    hidden_wide = features.astype(jnp.float32)
    normed = (
        hidden_wide
        * lax.rsqrt(jnp.mean(hidden_wide * hidden_wide, axis=-1, keepdims=True) + epsilon)
    ).astype(jnp.bfloat16)
    fresh_key = exchange(key_weight, "rep", owner_rank)
    fresh_value = exchange(value_weight, "rep", owner_rank)
    fresh_query = exchange(query_weight, "rep", owner_rank)
    edges = [out_weight.shape[1] * cut // 8 for cut in OUT_CUTS]
    spans = list(zip(edges[:-1], edges[1:]))
    out_pieces = [exchange(out_weight[:, low:high], "rep", owner_rank) for low, high in spans]
    fresh_out = out_weight
    for (low, high), piece in zip(spans, out_pieces):
        fresh_out = lax.dynamic_update_slice(fresh_out, piece, (0, low, 0))
    query_rows = fresh_query[0]
    key_rows = fresh_key[0]
    value_rows = fresh_value[0]
    seqs = normed.shape[0]
    query_width = query_rows.shape[1]
    key_width = key_rows.shape[1]
    token_block = lax.all_to_all(normed, "fs", split_axis=1, concat_axis=0, tiled=True)
    groups = lax.axis_size("fs")
    joined = scatter_sum(
        jnp.concatenate(
            [
                jnp.dot(token_block, query_rows, preferred_element_type=jnp.float32),
                jnp.dot(token_block, key_rows, preferred_element_type=jnp.float32),
                jnp.dot(token_block, value_rows, preferred_element_type=jnp.float32),
            ],
            axis=1,
        ).reshape(groups, seqs, query_width + 2 * key_width),
        "fs",
    )
    query_proj = joined[:, :query_width]
    key_proj = joined[:, query_width : query_width + key_width]
    value_proj = joined[:, query_width + key_width :]
    q_heads = query_proj.shape[1] // DH
    kv_heads = key_proj.shape[1] // DH
    query_rot = rotate(query_proj.reshape(seqs, q_heads, DH), lengths).astype(jnp.bfloat16)
    query_rot = query_rot.reshape(seqs, kv_heads, q_heads // kv_heads, DH)
    key_new = rotate(key_proj.reshape(seqs, kv_heads, DH), lengths).astype(jnp.bfloat16)
    value_new = value_proj.astype(jnp.bfloat16).reshape(seqs, kv_heads, DH)
    context = attend(query_rot, key_new, value_new, cache_key, cache_value, lengths)
    context = context.astype(jnp.bfloat16).reshape(seqs, q_heads * DH)
    group_context = gather(context, "fs", 0)
    partial_out = 0.0
    for (low, high), piece in zip(spans, out_pieces):
        partial_out = partial_out + jnp.dot(
            group_context[:, low:high],
            piece[0],
            preferred_element_type=jnp.float32,
        )
    terms = lax.all_to_all(partial_out, "fs", split_axis=0, concat_axis=1, tiled=True)
    model_groups = lax.axis_size("tp")
    terms = terms.reshape(seqs, model_groups, -1).transpose(1, 0, 2)
    summed = scatter_sum(terms, "tp")
    mixed = (summed + hidden.astype(jnp.float32)).astype(jnp.bfloat16)
    return (
        mixed,
        key_new.reshape(seqs, kv_heads * DH),
        value_new.reshape(seqs, kv_heads * DH),
        fresh_query,
        fresh_key,
        fresh_value,
        fresh_out,
    )


def solution(mesh):
    return jax.shard_map(
        local,
        mesh=mesh,
        in_specs=(
            P(("rep", "fs"), "tp"),
            P(("rep", "fs"), None, "tp"),
            P(("rep", "fs"), None, "tp"),
            P(("rep", "fs")),
            P(),
            P("rep", "fs", "tp"),
            P("rep", "fs", "tp"),
            P("rep", "fs", "tp"),
            P("rep", "tp", "fs"),
        ),
        out_specs=(
            P(("rep", "fs"), "tp"),
            P(("rep", "fs"), "tp"),
            P(("rep", "fs"), "tp"),
            P("rep", "fs", "tp"),
            P("rep", "fs", "tp"),
            P("rep", "fs", "tp"),
            P("rep", "tp", "fs"),
        ),
        check_vma=False,
    )
```

```python
import functools

import jax
import jax.numpy as jnp
from jax import lax
from jax.experimental import pallas as pl
from jax.experimental.pallas import tpu as pltpu
from jax.sharding import PartitionSpec as P

DH = 128


rope_base = 500000.0
epsilon = 1e-05


def exchange(shard, axis, root):
    size = lax.axis_size(axis)
    rank = lax.axis_index(axis)
    if size & (size - 1):
        return lax.psum(jnp.where(rank == root, shard, jnp.zeros_like(shard)), axis)
    away = jnp.bitwise_xor(rank, root)
    step = 1
    while step < size:
        pairs = [(i, i ^ step) for i in range(size)]
        received = lax.ppermute(shard, axis, pairs)
        takes = (away >= step) & (away < 2 * step)
        shard = jnp.where(takes, received, shard)
        step *= 2
    return shard


OUT_CUTS = (0, 4, 7, 8)


def gather(shard, axis, dim):
    size = lax.axis_size(axis)
    copies = jnp.broadcast_to(shard[None], (size,) + shard.shape)
    pieces = lax.all_to_all(copies, axis, split_axis=0, concat_axis=0, tiled=True)
    return jnp.concatenate([pieces[i] for i in range(size)], axis=dim)


def scatter_sum(terms, axis):
    return jnp.sum(lax.all_to_all(terms, axis, split_axis=0, concat_axis=0, tiled=True), axis=0)


MESH = pl.DeviceIdType.MESH


def deliver_kernel(ratio, part, out, land, send, recv, own_sem):
    member = lax.axis_index("fs")
    model = lax.axis_index("tp")
    count = part.shape[0]
    source = model // ratio
    inner = source == member
    barrier = pltpu.get_barrier_semaphore()
    for i in range(count):

        @pl.when(jnp.logical_not(inner & (model == i)))
        def _():
            pl.semaphore_signal(
                barrier, inc=1, device_id={"tp": i, "fs": source}, device_id_type=MESH
            )

    @pl.when(inner)
    def _():
        pl.semaphore_wait(barrier, count - 1)

    @pl.when(jnp.logical_not(inner))
    def _():
        pl.semaphore_wait(barrier, count)

    def copy(k):
        return pltpu.make_async_remote_copy(
            src_ref=part.at[k],
            dst_ref=land.at[model],
            send_sem=send.at[k],
            recv_sem=recv.at[model],
            device_id={"tp": member * ratio + k % ratio, "fs": k // ratio},
            device_id_type=MESH,
        )

    def here(k):
        return (member == k // ratio) & (model == member * ratio + k % ratio)

    def keep(k):
        return pltpu.make_async_copy(part.at[k], land.at[model], own_sem)

    for k in range(count):

        @pl.when(jnp.logical_not(here(k)))
        def _():
            copy(k).start()

        @pl.when(here(k))
        def _():
            keep(k).start()

    for k in range(count):

        @pl.when(jnp.logical_not(here(k)))
        def _():
            copy(k).wait_send()

        @pl.when(here(k))
        def _():
            keep(k).wait()

    for i in range(count):

        @pl.when(jnp.logical_not(inner & (model == i)))
        def _():
            pltpu.make_async_remote_copy(
                src_ref=part.at[0],
                dst_ref=land.at[i],
                send_sem=send.at[0],
                recv_sem=recv.at[i],
                device_id={"tp": i, "fs": source},
                device_id_type=MESH,
            ).wait_recv()

    total = land[0]
    for i in range(1, count):
        total = total + land[i]
    out[...] = total


def deliver(partial_out, seqs):
    members = lax.axis_size("fs")
    models = lax.axis_size("tp")
    if models % members:
        terms = lax.all_to_all(partial_out, "fs", split_axis=0, concat_axis=1, tiled=True)
        return scatter_sum(terms.reshape(seqs, models, -1).transpose(1, 0, 2), "tp")
    ratio = models // members
    width = partial_out.shape[1] // ratio
    parts = partial_out.reshape(members, seqs, ratio, width).transpose(0, 2, 1, 3)
    return pl.pallas_call(
        functools.partial(deliver_kernel, ratio),
        out_shape=jax.ShapeDtypeStruct((seqs, width), jnp.float32),
        in_specs=[pl.BlockSpec(memory_space=pltpu.VMEM)],
        out_specs=pl.BlockSpec(memory_space=pltpu.VMEM),
        scratch_shapes=[
            pltpu.VMEM((models, seqs, width), jnp.float32),
            pltpu.SemaphoreType.DMA((models,)),
            pltpu.SemaphoreType.DMA((models,)),
            pltpu.SemaphoreType.DMA,
        ],
        compiler_params=pltpu.CompilerParams(collective_id=0, has_side_effects=True),
        name="deliver",
    )(parts.reshape(models, seqs, width))


def rotate(heads, positions):
    half_dim = heads.shape[-1] // 2
    frequency = rope_base ** (-(jnp.arange(half_dim, dtype=jnp.float32) * 2.0 / heads.shape[-1]))
    angles = positions.astype(jnp.float32)[:, None] * frequency[None, :]
    cosine = jnp.cos(angles)[:, None, :]
    sine_part = jnp.sin(angles)[:, None, :]
    first_half = heads[..., :half_dim]
    second_half = heads[..., half_dim:]
    return jnp.concatenate(
        [
            first_half * cosine - second_half * sine_part,
            second_half * cosine + first_half * sine_part,
        ],
        axis=-1,
    )


def attend(query, own_key, own_value, cache_key, cache_value, lengths):
    seqs, span, _ = cache_key.shape
    kv_local = query.shape[1]
    head_size = query.shape[3]
    keys_view = cache_key.reshape(seqs, span, kv_local, head_size)
    values_view = cache_value.reshape(seqs, span, kv_local, head_size)
    scale = head_size ** (-0.5)
    scores = (
        jnp.einsum("shgd,sthd->shgt", query, keys_view, preferred_element_type=jnp.float32) * scale
    )
    own_score = (
        jnp.einsum("shgd,shd->shg", query, own_key, preferred_element_type=jnp.float32) * scale
    )
    live = (jnp.arange(span, dtype=jnp.int32)[None, :] < lengths[:, None])[:, None, None, :]
    masked = jnp.where(live, scores, -jnp.inf)
    row_max = jnp.maximum(jnp.max(masked, axis=-1), own_score)
    weights = jnp.where(live, jnp.exp(scores - row_max[..., None]), 0.0)
    own_weight = jnp.exp(own_score - row_max)
    denominator = jnp.sum(weights, axis=-1) + own_weight
    probs = (weights / denominator[..., None]).astype(jnp.bfloat16)
    own_prob = (own_weight / denominator).astype(jnp.bfloat16)
    context = jnp.einsum("shgt,sthd->shgd", probs, values_view, preferred_element_type=jnp.float32)
    return (
        context
        + own_prob.astype(jnp.float32)[..., None] * own_value.astype(jnp.float32)[:, :, None, :]
    )


def local(
    hidden,
    cache_key,
    cache_value,
    lengths,
    owner,
    query_weight,
    key_weight,
    value_weight,
    out_weight,
):
    owner_rank = owner[0] % lax.axis_size("rep")
    features = gather(hidden, "tp", 1)
    hidden_wide = features.astype(jnp.float32)
    normed = (
        hidden_wide
        * lax.rsqrt(jnp.mean(hidden_wide * hidden_wide, axis=-1, keepdims=True) + epsilon)
    ).astype(jnp.bfloat16)
    fresh_key = exchange(key_weight, "rep", owner_rank)
    fresh_value = exchange(value_weight, "rep", owner_rank)
    fresh_query = exchange(query_weight, "rep", owner_rank)
    edges = [out_weight.shape[1] * cut // 8 for cut in OUT_CUTS]
    spans = list(zip(edges[:-1], edges[1:]))
    held_pieces = lax.optimization_barrier([out_weight[:, low:high] for low, high in spans])
    out_pieces = [exchange(piece, "rep", owner_rank) for piece in held_pieces]
    normed, fresh_out = lax.optimization_barrier((normed, out_weight))
    for (low, high), piece in zip(spans, out_pieces):
        fresh_out = lax.dynamic_update_slice(fresh_out, piece, (0, low, 0))
    query_rows = fresh_query[0]
    key_rows = fresh_key[0]
    value_rows = fresh_value[0]
    seqs = normed.shape[0]
    query_width = query_rows.shape[1]
    key_width = key_rows.shape[1]
    token_block = lax.all_to_all(normed, "fs", split_axis=1, concat_axis=0, tiled=True)
    groups = lax.axis_size("fs")
    joined = scatter_sum(
        jnp.concatenate(
            [
                jnp.dot(token_block, query_rows, preferred_element_type=jnp.float32),
                jnp.dot(token_block, key_rows, preferred_element_type=jnp.float32),
                jnp.dot(token_block, value_rows, preferred_element_type=jnp.float32),
            ],
            axis=1,
        ).reshape(groups, seqs, query_width + 2 * key_width),
        "fs",
    )
    query_proj = joined[:, :query_width]
    key_proj = joined[:, query_width : query_width + key_width]
    value_proj = joined[:, query_width + key_width :]
    q_heads = query_proj.shape[1] // DH
    kv_heads = key_proj.shape[1] // DH
    query_rot = rotate(query_proj.reshape(seqs, q_heads, DH), lengths).astype(jnp.bfloat16)
    query_rot = query_rot.reshape(seqs, kv_heads, q_heads // kv_heads, DH)
    key_new = rotate(key_proj.reshape(seqs, kv_heads, DH), lengths).astype(jnp.bfloat16)
    value_new = value_proj.astype(jnp.bfloat16).reshape(seqs, kv_heads, DH)
    context = attend(query_rot, key_new, value_new, cache_key, cache_value, lengths)
    context = context.astype(jnp.bfloat16).reshape(seqs, q_heads * DH)
    group_context = gather(context, "fs", 0)
    partial_out = None
    for (low, high), piece in zip(spans, out_pieces):
        term = jnp.dot(
            group_context[:, low:high],
            piece[0],
            preferred_element_type=jnp.float32,
        )
        if partial_out is None:
            partial_out = term
        else:
            partial_out = lax.optimization_barrier(partial_out) + term
    summed = deliver(partial_out, seqs)
    mixed = (summed + hidden.astype(jnp.float32)).astype(jnp.bfloat16)
    return (
        mixed,
        key_new.reshape(seqs, kv_heads * DH),
        value_new.reshape(seqs, kv_heads * DH),
        fresh_query,
        fresh_key,
        fresh_value,
        fresh_out,
    )


def solution(mesh):
    return jax.shard_map(
        local,
        mesh=mesh,
        in_specs=(
            P(("rep", "fs"), "tp"),
            P(("rep", "fs"), None, "tp"),
            P(("rep", "fs"), None, "tp"),
            P(("rep", "fs")),
            P(),
            P("rep", "fs", "tp"),
            P("rep", "fs", "tp"),
            P("rep", "fs", "tp"),
            P("rep", "tp", "fs"),
        ),
        out_specs=(
            P(("rep", "fs"), "tp"),
            P(("rep", "fs"), "tp"),
            P(("rep", "fs"), "tp"),
            P("rep", "fs", "tp"),
            P("rep", "fs", "tp"),
            P("rep", "fs", "tp"),
            P("rep", "tp", "fs"),
        ),
        check_vma=False,
    )
```

```python
import functools

import jax
import jax.numpy as jnp
from jax import lax
from jax.experimental import pallas as pl
from jax.experimental.pallas import tpu as pltpu
from jax.sharding import PartitionSpec as P

DH = 128


rope_base = 500000.0
epsilon = 1e-05


def exchange(shard, axis, root):
    size = lax.axis_size(axis)
    rank = lax.axis_index(axis)
    if size & (size - 1):
        return lax.psum(jnp.where(rank == root, shard, jnp.zeros_like(shard)), axis)
    away = jnp.bitwise_xor(rank, root)
    step = 1
    while step < size:
        pairs = [(i, i ^ step) for i in range(size)]
        received = lax.ppermute(shard, axis, pairs)
        takes = (away >= step) & (away < 2 * step)
        shard = jnp.where(takes, received, shard)
        step *= 2
    return shard


OUT_CUTS = (0, 4, 7, 8)


def gather(shard, axis, dim):
    size = lax.axis_size(axis)
    copies = jnp.broadcast_to(shard[None], (size,) + shard.shape)
    pieces = lax.all_to_all(copies, axis, split_axis=0, concat_axis=0, tiled=True)
    return jnp.concatenate([pieces[i] for i in range(size)], axis=dim)


def scatter_sum(terms, axis):
    return jnp.sum(lax.all_to_all(terms, axis, split_axis=0, concat_axis=0, tiled=True), axis=0)


MESH = pl.DeviceIdType.MESH


def deliver_kernel(ratio, part, out, land, send, recv, own_sem):
    member = lax.axis_index("fs")
    model = lax.axis_index("tp")
    count = part.shape[0]
    source = model // ratio
    inner = source == member
    barrier = pltpu.get_barrier_semaphore()
    for i in range(count):

        @pl.when(jnp.logical_not(inner & (model == i)))
        def _():
            pl.semaphore_signal(
                barrier, inc=1, device_id={"tp": i, "fs": source}, device_id_type=MESH
            )

    @pl.when(inner)
    def _():
        pl.semaphore_wait(barrier, count - 1)

    @pl.when(jnp.logical_not(inner))
    def _():
        pl.semaphore_wait(barrier, count)

    def copy(k):
        return pltpu.make_async_remote_copy(
            src_ref=part.at[k],
            dst_ref=land.at[model],
            send_sem=send.at[k],
            recv_sem=recv.at[model],
            device_id={"tp": member * ratio + k % ratio, "fs": k // ratio},
            device_id_type=MESH,
        )

    def here(k):
        return (member == k // ratio) & (model == member * ratio + k % ratio)

    def keep(k):
        return pltpu.make_async_copy(part.at[k], land.at[model], own_sem)

    for k in range(count):

        @pl.when(jnp.logical_not(here(k)))
        def _():
            copy(k).start()

        @pl.when(here(k))
        def _():
            keep(k).start()

    for k in range(count):

        @pl.when(jnp.logical_not(here(k)))
        def _():
            copy(k).wait_send()

        @pl.when(here(k))
        def _():
            keep(k).wait()

    for i in range(count):

        @pl.when(jnp.logical_not(inner & (model == i)))
        def _():
            pltpu.make_async_remote_copy(
                src_ref=part.at[0],
                dst_ref=land.at[i],
                send_sem=send.at[0],
                recv_sem=recv.at[i],
                device_id={"tp": i, "fs": source},
                device_id_type=MESH,
            ).wait_recv()

    total = land[0]
    for i in range(1, count):
        total = total + land[i]
    out[...] = total


def deliver(partial_out, seqs):
    members = lax.axis_size("fs")
    models = lax.axis_size("tp")
    if models % members:
        terms = lax.all_to_all(partial_out, "fs", split_axis=0, concat_axis=1, tiled=True)
        return scatter_sum(terms.reshape(seqs, models, -1).transpose(1, 0, 2), "tp")
    ratio = models // members
    width = partial_out.shape[1] // ratio
    parts = partial_out.reshape(members, seqs, ratio, width).transpose(0, 2, 1, 3)
    return pl.pallas_call(
        functools.partial(deliver_kernel, ratio),
        out_shape=jax.ShapeDtypeStruct((seqs, width), jnp.float32),
        in_specs=[pl.BlockSpec(memory_space=pltpu.VMEM)],
        out_specs=pl.BlockSpec(memory_space=pltpu.VMEM),
        scratch_shapes=[
            pltpu.VMEM((models, seqs, width), jnp.float32),
            pltpu.SemaphoreType.DMA((models,)),
            pltpu.SemaphoreType.DMA((models,)),
            pltpu.SemaphoreType.DMA,
        ],
        compiler_params=pltpu.CompilerParams(collective_id=0, has_side_effects=True),
        name="deliver",
    )(parts.reshape(models, seqs, width))


def rotate(heads, positions):
    half_dim = heads.shape[-1] // 2
    frequency = rope_base ** (-(jnp.arange(half_dim, dtype=jnp.float32) * 2.0 / heads.shape[-1]))
    angles = positions.astype(jnp.float32)[:, None] * frequency[None, :]
    cosine = jnp.cos(angles)[:, None, :]
    sine_part = jnp.sin(angles)[:, None, :]
    first_half = heads[..., :half_dim]
    second_half = heads[..., half_dim:]
    return jnp.concatenate(
        [
            first_half * cosine - second_half * sine_part,
            second_half * cosine + first_half * sine_part,
        ],
        axis=-1,
    )


def attend(query, own_key, own_value, cache_key, cache_value, lengths):
    seqs, span, _ = cache_key.shape
    kv_local = query.shape[1]
    head_size = query.shape[3]
    keys_view = cache_key.reshape(seqs, span, kv_local, head_size)
    values_view = cache_value.reshape(seqs, span, kv_local, head_size)
    scale = head_size ** (-0.5)
    scores = (
        jnp.einsum("shgd,sthd->shgt", query, keys_view, preferred_element_type=jnp.float32) * scale
    )
    own_score = (
        jnp.einsum("shgd,shd->shg", query, own_key, preferred_element_type=jnp.float32) * scale
    )
    live = (jnp.arange(span, dtype=jnp.int32)[None, :] < lengths[:, None])[:, None, None, :]
    masked = jnp.where(live, scores, -jnp.inf)
    row_max = jnp.maximum(jnp.max(masked, axis=-1), own_score)
    weights = jnp.where(live, jnp.exp(scores - row_max[..., None]), 0.0)
    own_weight = jnp.exp(own_score - row_max)
    denominator = jnp.sum(weights, axis=-1) + own_weight
    probs = (weights / denominator[..., None]).astype(jnp.bfloat16)
    own_prob = (own_weight / denominator).astype(jnp.bfloat16)
    context = jnp.einsum("shgt,sthd->shgd", probs, values_view, preferred_element_type=jnp.float32)
    return (
        context
        + own_prob.astype(jnp.float32)[..., None] * own_value.astype(jnp.float32)[:, :, None, :]
    )


def local(
    hidden,
    cache_key,
    cache_value,
    lengths,
    owner,
    query_weight,
    key_weight,
    value_weight,
    out_weight,
):
    owner_rank = owner[0] % lax.axis_size("rep")
    features = gather(hidden, "tp", 1)
    hidden_wide = features.astype(jnp.float32)
    normed = (
        hidden_wide
        * lax.rsqrt(jnp.mean(hidden_wide * hidden_wide, axis=-1, keepdims=True) + epsilon)
    ).astype(jnp.bfloat16)
    fresh_key = exchange(key_weight, "rep", owner_rank)
    fresh_value = exchange(value_weight, "rep", owner_rank)
    fresh_query = exchange(query_weight, "rep", owner_rank)
    edges = [out_weight.shape[1] * cut // 8 for cut in OUT_CUTS]
    spans = list(zip(edges[:-1], edges[1:]))
    held_pieces = lax.optimization_barrier([out_weight[:, low:high] for low, high in spans])
    out_pieces = [exchange(piece, "rep", owner_rank) for piece in held_pieces]
    first_rows = edges[1]
    rows = lax.broadcasted_iota(jnp.int32, out_weight.shape, 1)
    padded = jnp.pad(out_pieces[0], ((0, 0), (0, out_weight.shape[1] - first_rows), (0, 0)))
    fresh_out = jnp.where(rows < first_rows, padded, out_weight)
    for (low, high), piece in zip(spans[1:], out_pieces[1:]):
        fresh_out = lax.dynamic_update_slice(fresh_out, piece, (0, low, 0))
    query_rows = fresh_query[0]
    key_rows = fresh_key[0]
    value_rows = fresh_value[0]
    seqs = normed.shape[0]
    query_width = query_rows.shape[1]
    key_width = key_rows.shape[1]
    token_block = lax.all_to_all(normed, "fs", split_axis=1, concat_axis=0, tiled=True)
    groups = lax.axis_size("fs")
    joined = scatter_sum(
        jnp.concatenate(
            [
                jnp.dot(token_block, query_rows, preferred_element_type=jnp.float32),
                jnp.dot(token_block, key_rows, preferred_element_type=jnp.float32),
                jnp.dot(token_block, value_rows, preferred_element_type=jnp.float32),
            ],
            axis=1,
        ).reshape(groups, seqs, query_width + 2 * key_width),
        "fs",
    )
    query_proj = joined[:, :query_width]
    key_proj = joined[:, query_width : query_width + key_width]
    value_proj = joined[:, query_width + key_width :]
    q_heads = query_proj.shape[1] // DH
    kv_heads = key_proj.shape[1] // DH
    query_rot = rotate(query_proj.reshape(seqs, q_heads, DH), lengths).astype(jnp.bfloat16)
    query_rot = query_rot.reshape(seqs, kv_heads, q_heads // kv_heads, DH)
    key_new = rotate(key_proj.reshape(seqs, kv_heads, DH), lengths).astype(jnp.bfloat16)
    value_new = value_proj.astype(jnp.bfloat16).reshape(seqs, kv_heads, DH)
    context = attend(query_rot, key_new, value_new, cache_key, cache_value, lengths)
    context = context.astype(jnp.bfloat16).reshape(seqs, q_heads * DH)
    group_context = gather(context, "fs", 0)
    partial_out = None
    for (low, high), piece in zip(spans, out_pieces):
        term = jnp.dot(
            group_context[:, low:high],
            piece[0],
            preferred_element_type=jnp.float32,
        )
        if partial_out is None:
            partial_out = term
        else:
            partial_out = lax.optimization_barrier(partial_out) + term
    summed = deliver(partial_out, seqs)
    mixed = (summed + hidden.astype(jnp.float32)).astype(jnp.bfloat16)
    return (
        mixed,
        key_new.reshape(seqs, kv_heads * DH),
        value_new.reshape(seqs, kv_heads * DH),
        fresh_query,
        fresh_key,
        fresh_value,
        fresh_out,
    )


def solution(mesh):
    return jax.shard_map(
        local,
        mesh=mesh,
        in_specs=(
            P(("rep", "fs"), "tp"),
            P(("rep", "fs"), None, "tp"),
            P(("rep", "fs"), None, "tp"),
            P(("rep", "fs")),
            P(),
            P("rep", "fs", "tp"),
            P("rep", "fs", "tp"),
            P("rep", "fs", "tp"),
            P("rep", "tp", "fs"),
        ),
        out_specs=(
            P(("rep", "fs"), "tp"),
            P(("rep", "fs"), "tp"),
            P(("rep", "fs"), "tp"),
            P("rep", "fs", "tp"),
            P("rep", "fs", "tp"),
            P("rep", "fs", "tp"),
            P("rep", "tp", "fs"),
        ),
        check_vma=False,
    )
```
